32 devices in a mesh: grp: 4 (over y, x), dev: 8 (over z, core).
Axes of the slice: x: 2, y: 2, z: 4, core: 2. Of those that a mesh axis runs over, the one named last changes fastest.
Arguments:
- captions: bfloat16 [8, 64, 4096], P('dev', 'grp'), may hold values from -6 to 6
- kv_weight: bfloat16 [4096, 2048], P('grp'), may hold values from -0.09375 to 0.09375
- image_tokens: bfloat16 [128, 256, 2048], P(('grp', 'dev')), may hold values from -28 to 28
- q_weight: bfloat16 [2048, 1024], replicated, may hold values from -0.125 to 0.125
- context_grad: bfloat16 [128, 256, 1024], P(('grp', 'dev')), may hold values from -6 to 6
- sample_prompt: int32 [128], replicated, may hold values from 0 to 7
- caption_len: int32 [8], replicated, may hold values from 8 to 64
Outputs:
- context: bfloat16 [128, 256, 1024], P(('grp', 'dev'))
- image_grad: bfloat16 [128, 256, 2048], P(('grp', 'dev'))
- caption_grad: float32 [8, 64, 4096], P('dev', 'grp')
The draws below stay inside these ranges and needn't reach their ends.
Inputs may be any that keep to these rules, and one draw needn't show every extreme that they name: `sample_prompt`: sample s belongs to the device at position s // 4 of the devices taken with grp slowest; a prompt may have no samples.
All inputs are finite; a program needn't handle non-finite values.
Results may differ from the reference program's by a relative error of at most 0.008.
Values may be sent and summed in bfloat16 or wider, within the bound.
No kernel may reach another device: no remote copies, remote signals or barrier semaphores. Data moves between devices by JAX's collectives and lax.ppermute only.
A program may use at most 128 MiB of HBM per device.

```python
import math
import jax
import jax.numpy as jnp
import numpy as np
from jax import lax

E = 4096
C = 2048
HEADS = 8
HD = 128
INNER = 1024
L = 64
IMG = 256
PROMPTS = 8
SAMPLES = 128


def draw_image_tokens(key, part):
    first_key = jax.random.fold_in(jax.random.fold_in(key, 17), 0)
    return jnp.clip(jax.random.normal(first_key, (SAMPLES, IMG, C), jnp.float32), -6.0, 6.0).astype(jnp.bfloat16)


def plant(drawn, rng, least, high):
    extent = drawn.shape
    spot = [jax.random.randint(jax.random.fold_in(rng, axis), (), 0, extent[axis]) for axis in range(len(extent))]
    drawn = drawn.at[tuple(spot)].set(least)
    longest = extent.index(max(extent))
    spot[longest] = (spot[longest] + 1) % extent[longest]
    return drawn.at[tuple(spot)].set(high)


def levels(own_key, extent, cuts, smallest, largest):
    def one(position, shards_of):
        steps = jax.random.uniform(jax.random.fold_in(jax.random.fold_in(own_key, 6), position), (shards_of,), jnp.float32, smallest / len(cuts), largest / len(cuts))
        return jnp.repeat(jnp.exp(steps), extent[position] // shards_of).reshape((-1,) + (1,) * (len(extent) - position - 1))

    loudness = one(*cuts[0])
    for cut in cuts[1:]:
        loudness = loudness * one(*cut)
    return loudness


def rank_bounds(count, skew):
    portions = [(1 << 20) // math.isqrt(rank ** skew) + 1 for rank in range(1, count + 1)]
    deviation = 1 + sum(portions) // (1 << 30)
    return np.cumsum(np.array([max(1, weight // deviation) for weight in portions]))


def ranked(rng, shape, amount, slope):
    listing = rank_bounds(amount, slope)
    pick = jax.random.randint(jax.random.fold_in(rng, 1), shape, 0, int(listing[amount - 1]))
    grade = jnp.searchsorted(jnp.asarray(listing, jnp.int32), pick, side="right")
    return jax.random.permutation(jax.random.fold_in(rng, 2), amount)[grade].astype(jnp.int32)


def scatter_about(stream_key, extent, spread, limit, cuts=(), held_as=jnp.bfloat16):
    level = levels(stream_key, extent, cuts, -0.22, 0.18) if cuts else 1.0
    entries = jax.random.normal(stream_key, extent, jnp.float32) * spread * level
    return jnp.minimum(jnp.maximum(entries, -limit), limit).astype(held_as)


def setup_inputs(seed: int = 0) -> dict:
    streams_of = jax.random.split(jax.random.key(seed), 8)
    return {
        "captions": scatter_about(streams_of[0], (PROMPTS, L, E), 1.0, 6.0, ((0, 8), (1, 4))),
        "kv_weight": scatter_about(streams_of[1], (E, 2 * INNER), E ** -0.5, 0.09375, ((0, 4),)),
        "image_tokens": draw_image_tokens(jax.random.fold_in(streams_of[7], 71), 0),
        "q_weight": scatter_about(streams_of[3], (C, INNER), C ** -0.5, 0.125),
        "context_grad": scatter_about(streams_of[4], (SAMPLES, IMG, INNER), 1.0, 6.0, ((0, 32),)),
        "sample_prompt": plant(ranked(streams_of[5], (SAMPLES,), PROMPTS, 2), jax.random.fold_in(streams_of[5], 3), 0, PROMPTS - 1).astype(jnp.int32),
        "caption_len": plant(jax.random.randint(streams_of[6], (PROMPTS,), L // 8, L + 1), jax.random.fold_in(streams_of[6], 1), L // 8, L).astype(jnp.int32),
    }


NEG_FILL = -1e+30

def attend_one(queries, key_rows, value_rows, live, grad_rows):
    score_scale = 1.0 / math.sqrt(HD)
    scores = jnp.einsum('ihd,jhd->hij', queries.astype(jnp.float32), key_rows.astype(jnp.float32)) * score_scale
    scores = jnp.where(live[None, None, :], scores, NEG_FILL)
    top_score = lax.optimization_barrier(jnp.max(scores, axis=-1, keepdims=True))
    expd = jnp.exp(scores - top_score)
    soft = expd / lax.optimization_barrier(jnp.sum(expd, axis=-1, keepdims=True))
    soft_b = soft.astype(jnp.bfloat16)
    context = jnp.einsum('hij,jhd->ihd', soft_b.astype(jnp.float32), value_rows.astype(jnp.float32)).astype(jnp.bfloat16)
    d_soft = jnp.einsum('ihd,jhd->hij', grad_rows.astype(jnp.float32), value_rows.astype(jnp.float32))
    d_values = jnp.einsum('hij,ihd->jhd', soft_b.astype(jnp.float32), grad_rows.astype(jnp.float32))
    d_scores = (soft * (d_soft - lax.optimization_barrier(jnp.sum(d_soft * soft, axis=-1, keepdims=True))) * score_scale).astype(jnp.bfloat16)
    d_keys = jnp.einsum('hij,ihd->jhd', d_scores.astype(jnp.float32), queries.astype(jnp.float32))
    d_queries = jnp.einsum('hij,jhd->ihd', d_scores.astype(jnp.float32), key_rows.astype(jnp.float32)).astype(jnp.bfloat16)
    return (context, d_queries, d_keys, d_values)

def reference(captions, kv_weight, image_tokens, q_weight, context_grad, sample_prompt, caption_len):
    kv_all = jnp.dot(captions.reshape(PROMPTS * L, E), kv_weight, preferred_element_type=jnp.float32)
    kv_all = kv_all.astype(jnp.bfloat16).reshape(PROMPTS, L, 2 * INNER)
    positions = jnp.arange(L, dtype=jnp.int32)

    def one_sample(carry, inputs):
        tokens_one, grad_one, prompt_id = inputs
        prompt_id = prompt_id.astype(jnp.int32)
        kv_rows = lax.dynamic_index_in_dim(kv_all, prompt_id, 0, keepdims=False)
        length = lax.dynamic_index_in_dim(caption_len, prompt_id, 0, keepdims=False)
        queries = jnp.dot(tokens_one, q_weight, preferred_element_type=jnp.float32).astype(jnp.bfloat16)
        queries = queries.reshape(IMG, HEADS, HD)
        key_rows = kv_rows[:, :INNER].reshape(L, HEADS, HD)
        value_rows = kv_rows[:, INNER:].reshape(L, HEADS, HD)
        live = positions < length
        context, d_queries, d_keys, d_values = attend_one(queries, key_rows, value_rows, live, grad_one.reshape(IMG, HEADS, HD))
        image_grad = jnp.dot(d_queries.reshape(IMG, INNER), q_weight.T, preferred_element_type=jnp.float32).astype(jnp.bfloat16)
        grad_kv = jnp.concatenate([d_keys.reshape(L, INNER), d_values.reshape(L, INNER)], axis=1)
        current = lax.dynamic_index_in_dim(carry, prompt_id, 0, keepdims=False)
        carry = lax.dynamic_update_index_in_dim(carry, current + grad_kv, prompt_id, 0)
        return (carry, (context.reshape(IMG, INNER), image_grad))
    start_sums = jnp.zeros((PROMPTS, L, 2 * INNER), jnp.float32)
    kv_grad, (context, image_grad) = lax.scan(one_sample, start_sums, (image_tokens, context_grad, sample_prompt))
    kv_grad_b = kv_grad.astype(jnp.bfloat16).reshape(PROMPTS * L, 2 * INNER)
    caption_grad = jnp.dot(kv_grad_b, kv_weight.T, preferred_element_type=jnp.float32).reshape(PROMPTS, L, E)
    return (context, image_grad, caption_grad)
```

```python
import functools
import math

import jax
import jax.numpy as jnp
from jax import lax
from jax.experimental import pallas as pl
from jax.experimental.pallas import tpu as pltpu
from jax.sharding import PartitionSpec as P

HEADS = 8
HD = 128
NEG_FILL = -1e30
F32 = jnp.float32
BF16 = jnp.bfloat16


def partner(x, axis, size, k):
    return lax.ppermute(x, axis, [(i, i ^ k) for i in range(size)])


def attend(ids, prompt_of, lens, queries, grads, own_kv, other_kv, shape):
    samp_dev, img_len, inner, n_grp, n_dev, block_len = shape
    full_len = n_grp * block_len
    scale = 1.0 / math.sqrt(HD)

    def prompt_at(s, ids_ref, prompt_ref):
        return prompt_ref[(ids_ref[0] * n_dev + ids_ref[1]) * samp_dev + s]

    def body(ids_ref, prompt_ref, len_ref, q_ref, g_ref, *refs):
        own = refs[:n_grp]
        other = refs[n_grp : 2 * n_grp]
        ctx_ref, dq_ref = refs[2 * n_grp : 2 * n_grp + 2]
        outs = refs[2 * n_grp + 2 : 3 * n_grp + 2]
        kv_ref = refs[3 * n_grp + 2]
        s = pl.program_id(0)
        prompt = prompt_at(s, ids_ref, prompt_ref)
        live_len = len_ref[prompt]
        flip = (prompt ^ ids_ref[1]) & 1

        @pl.when(flip == 0)
        def _():
            for k in range(n_grp):
                kv_ref[k * block_len : (k + 1) * block_len, :] = own[k][0]

        @pl.when(flip == 1)
        def _():
            for k in range(n_grp):
                kv_ref[k * block_len : (k + 1) * block_len, :] = other[k][0]

        row = lax.broadcasted_iota(jnp.int32, (full_len, 1), 0)
        token = ((row // block_len) ^ ids_ref[0]) * block_len + row % block_len
        live = token < live_len
        nt = (((1,), (1,)), ((), ()))
        tn = (((0,), (0,)), ((), ()))
        nn = (((1,), (0,)), ((), ()))

        def dot(a, b, dims):
            return lax.dot_general(a, b, dims, preferred_element_type=F32)

        for h in range(HEADS):
            cols = slice(h * HD, (h + 1) * HD)
            vcols = slice(inner + h * HD, inner + (h + 1) * HD)
            q = q_ref[:, cols]
            g = g_ref[:, cols]
            key = kv_ref[:, cols]
            val = kv_ref[:, vcols]
            scores = jnp.where(live, dot(key, q, nt) * scale, NEG_FILL)
            expd = jnp.exp(scores - jnp.max(scores, axis=0, keepdims=True))
            soft = expd * (1.0 / jnp.sum(expd, axis=0, keepdims=True))
            soft_b = soft.astype(BF16)
            d_soft = dot(val, g, nt)
            mean = jnp.sum(d_soft * soft, axis=0, keepdims=True)
            d_scores = (soft * (d_soft - mean) * scale).astype(BF16)
            ctx_ref[:, cols] = dot(soft_b, val, tn).astype(BF16)
            dq_ref[:, cols] = dot(d_scores, key, tn).astype(BF16)
            d_key = dot(d_scores, q, nn).astype(BF16)
            d_val = dot(soft_b, g, nn).astype(BF16)
            for k in range(n_grp):
                rows = slice(k * block_len, (k + 1) * block_len)
                outs[k][0, :, cols] = d_key[rows]
                outs[k][0, :, vcols] = d_val[rows]

    def kv_map(s, ids_ref, prompt_ref, len_ref):
        return ((prompt_at(s, ids_ref, prompt_ref) >> 1) ^ (ids_ref[1] >> 1), 0, 0)

    rows_spec = pl.BlockSpec((img_len, inner), lambda s, *_: (s, 0))
    kv_spec = pl.BlockSpec((1, block_len, 2 * inner), kv_map)
    out_spec = pl.BlockSpec((1, block_len, 2 * inner), lambda s, *_: (s, 0, 0))
    rows_shape = jax.ShapeDtypeStruct((samp_dev * img_len, inner), BF16)
    out_shape = jax.ShapeDtypeStruct((samp_dev, block_len, 2 * inner), BF16)
    return pl.pallas_call(
        body,
        grid_spec=pltpu.PrefetchScalarGridSpec(
            num_scalar_prefetch=3,
            grid=(samp_dev,),
            in_specs=[rows_spec, rows_spec] + [kv_spec] * (2 * n_grp),
            out_specs=[rows_spec, rows_spec] + [out_spec] * n_grp,
            scratch_shapes=[pltpu.VMEM((full_len, 2 * inner), BF16)],
        ),
        out_shape=[rows_shape, rows_shape] + [out_shape] * n_grp,
        name="attend",
    )(ids, prompt_of, lens, queries, grads, *own_kv, *other_kv)


def combine(ids, prompt_of, arrived, shape):
    samp_dev, n_grp, n_dev, block_len, width = shape
    chips = n_dev // 2

    def body(ids_ref, prompt_ref, *refs):
        same_ref, other_ref, acc_ref = refs[n_grp:]
        acc_ref[...] = jnp.zeros_like(acc_ref)
        for k in range(n_grp):
            base = ((ids_ref[0] ^ k) * n_dev + ids_ref[1]) * samp_dev
            for s in range(samp_dev):
                rel = prompt_ref[base + s] ^ ids_ref[1]
                slot = (rel & 1) * chips + (rel >> 1)
                acc_ref[slot] += refs[k][s].astype(F32)
        same_ref[...] = acc_ref[:chips]
        other_ref[...] = acc_ref[chips:].astype(BF16)

    vmem = pl.BlockSpec(memory_space=pltpu.VMEM)
    smem = pl.BlockSpec(memory_space=pltpu.SMEM)
    return pl.pallas_call(
        body,
        in_specs=[smem, smem] + [vmem] * n_grp,
        out_specs=[vmem, vmem],
        out_shape=[
            jax.ShapeDtypeStruct((chips, block_len, width), F32),
            jax.ShapeDtypeStruct((chips, block_len, width), BF16),
        ],
        scratch_shapes=[pltpu.VMEM((2 * chips, block_len, width), F32)],
        name="combine",
    )(ids, prompt_of, *arrived)


def shards(captions, kv_weight, image_tokens, q_weight, context_grad, sample_prompt, caption_len):
    n_grp = lax.axis_size("grp")
    n_dev = lax.axis_size("dev")
    grp_at = lax.axis_index("grp")
    dev_at = lax.axis_index("dev")
    samp_dev, img_len, width_img = image_tokens.shape
    _, block_len, width_cap = captions.shape
    inner = q_weight.shape[1]
    share = width_cap // n_grp
    chips = n_dev // 2
    ids = jnp.stack([grp_at, dev_at]).astype(jnp.int32)

    def over_grp(blocks):
        return [blocks[0]] + [partner(blocks[k], "grp", n_grp, k) for k in range(1, n_grp)]

    rows = captions.reshape(block_len, width_cap)
    pieces = [lax.dynamic_slice_in_dim(rows, (grp_at ^ k) * share, share, 1) for k in range(n_grp)]
    caption_share = jnp.concatenate(over_grp(pieces), axis=0)
    partial = jnp.dot(caption_share, kv_weight, preferred_element_type=F32)
    summed = over_grp([partial[k * block_len : (k + 1) * block_len] for k in range(n_grp)])
    kv_block = sum(summed[1:], summed[0]).astype(BF16)

    column = jnp.stack(
        [kv_block] + [partner(kv_block, "dev", n_dev, 2 * k) for k in range(1, chips)]
    )
    own_kv = over_grp([column] * n_grp)
    other_kv = [partner(x, "dev", n_dev, 1) for x in own_kv]

    queries = jnp.dot(
        image_tokens.reshape(samp_dev * img_len, width_img), q_weight, preferred_element_type=F32
    ).astype(BF16)
    context, d_queries, *d_kv = attend(
        ids,
        sample_prompt,
        caption_len,
        queries,
        context_grad.reshape(samp_dev * img_len, inner),
        own_kv,
        other_kv,
        (samp_dev, img_len, inner, n_grp, n_dev, block_len),
    )

    arrived = over_grp(d_kv)
    same, other = combine(
        ids, sample_prompt, arrived, (samp_dev, n_grp, n_dev, block_len, 2 * inner)
    )
    both = same + partner(other, "dev", n_dev, 1).astype(F32)
    kv_grad = both[0]
    for k in range(1, chips):
        kv_grad = kv_grad + partner(both[k].astype(BF16), "dev", n_dev, 2 * k).astype(F32)
    kv_grad_b = kv_grad.astype(BF16)
    grad_whole = jnp.concatenate(over_grp([kv_grad_b] * n_grp), axis=0)
    share_grad = lax.dot_general(
        grad_whole, kv_weight, (((1,), (1,)), ((), ())), preferred_element_type=F32
    )
    shares = over_grp([share_grad[k * block_len : (k + 1) * block_len] for k in range(n_grp)])
    caption_grad = jnp.zeros((block_len, width_cap), F32)
    for k in range(n_grp):
        caption_grad = lax.dynamic_update_slice_in_dim(
            caption_grad, shares[k], (grp_at ^ k) * share, 1
        )

    image_grad = lax.dot_general(
        d_queries, q_weight, (((1,), (1,)), ((), ())), preferred_element_type=F32
    ).astype(BF16)
    return (
        context.reshape(samp_dev, img_len, inner),
        image_grad.reshape(samp_dev, img_len, width_img),
        caption_grad[None],
    )


def solution(mesh):
    placed = (
        P("dev", "grp", None),
        P("grp", None),
        P(("grp", "dev"), None, None),
        P(),
        P(("grp", "dev"), None, None),
        P(),
        P(),
    )
    return jax.shard_map(
        shards,
        mesh=mesh,
        in_specs=placed,
        out_specs=(
            P(("grp", "dev"), None, None),
            P(("grp", "dev"), None, None),
            P("dev", "grp", None),
        ),
        check_vma=False,
    )
```

```python
import math

import jax
import jax.numpy as jnp
from jax import lax
from jax.experimental import pallas as pl
from jax.experimental.pallas import tpu as pltpu
from jax.sharding import PartitionSpec as P

HEADS = 8
HD = 128
NEG_FILL = -1e30
HALVES = 2
F32 = jnp.float32
BF16 = jnp.bfloat16
MIB = 1 << 20
NN = (((1,), (0,)), ((), ()))
NT = (((1,), (1,)), ((), ()))
TN = (((0,), (0,)), ((), ()))
VMEM = pl.BlockSpec(memory_space=pltpu.VMEM)
SMEM = pl.BlockSpec(memory_space=pltpu.SMEM)
ANY = pl.BlockSpec(memory_space=pl.ANY)
HBM = pl.BlockSpec(memory_space=pltpu.HBM)


def dot(a, b, dims):
    return lax.dot_general(a, b, dims, preferred_element_type=F32)


def partner(x, axis, size, k):
    return lax.ppermute(x, axis, [(i, i ^ k) for i in range(size)])


def shape_of(*dims, dtype=BF16):
    return jax.ShapeDtypeStruct(dims, dtype)


def params(limit):
    return pltpu.CompilerParams(vmem_limit_bytes=limit * MIB)


def cost(flops, size):
    return pl.CostEstimate(flops=flops, bytes_accessed=size, transcendentals=0)


def project(blocks, weight, dims, width):
    n = len(blocks)
    rows = blocks[0].shape[0]
    step = min(width, 512)

    def body(*refs):
        w_ref = refs[n]
        left = jnp.concatenate([r[...] for r in refs[:n]], axis=0)
        for start in range(0, width, step):
            cols = slice(start, start + step)
            w = w_ref[:, cols] if dims is NN else w_ref[cols, :]
            out = dot(left, w, dims)
            for k in range(n):
                refs[n + 1 + k][:, cols] = out[k * rows : (k + 1) * rows]

    return pl.pallas_call(
        body,
        in_specs=[VMEM] * (n + 1),
        out_specs=[VMEM] * n,
        out_shape=[shape_of(rows, width, dtype=F32)] * n,
        compiler_params=params(16),
        cost_estimate=cost(2 * n * rows * weight.size, weight.size * 2),
        name="project",
    )(*blocks, weight)


def far(x):
    return pltpu.with_memory_space_constraint(x, pltpu.HBM)


def fetch(arrays):
    n = len(arrays)

    def body(*refs):
        sem = refs[-1]
        copies = [pltpu.make_async_copy(refs[i], refs[n + i], sem.at[i]) for i in range(n)]
        for c in copies:
            c.start()
        for c in copies:
            c.wait()

    return pl.pallas_call(
        body,
        in_specs=[HBM] * n,
        out_specs=[VMEM] * n,
        out_shape=[shape_of(*a.shape) for a in arrays],
        scratch_shapes=[pltpu.SemaphoreType.DMA((n,))],
        compiler_params=params(16),
        cost_estimate=cost(0, sum(a.size for a in arrays) * 4),
        name="fetch",
    )(*[far(a) for a in arrays])


def query_product(tokens, weight, row0, rows):
    depth, width = weight.shape
    step = 256
    steps = rows // step

    def body(x_ref, w_ref, o_ref, x_buf, o_buf, x_sem, o_sem):
        def get(i):
            at = pl.ds(row0 + i * step, step)
            return pltpu.make_async_copy(x_ref.at[at, :], x_buf.at[i], x_sem.at[i])

        def put(i):
            at = pl.ds(i * step, step)
            return pltpu.make_async_copy(o_buf.at[i], o_ref.at[at, :], o_sem.at[i])

        for i in range(steps):
            get(i).start()
        for i in range(steps):
            get(i).wait()
            o_buf[i] = dot(x_buf[i], w_ref[...], NN).astype(BF16)
            put(i).start()
        for i in range(steps):
            put(i).wait()

    return pl.pallas_call(
        body,
        in_specs=[HBM, VMEM],
        out_specs=HBM,
        out_shape=pltpu.HBM((rows, width), BF16),
        scratch_shapes=[
            pltpu.VMEM((steps, step, depth), BF16),
            pltpu.VMEM((steps, step, width), BF16),
            pltpu.SemaphoreType.DMA((steps,)),
            pltpu.SemaphoreType.DMA((steps,)),
        ],
        compiler_params=params(24),
        cost_estimate=cost(2 * rows * depth * width, 2 * (rows * depth + depth * width)),
        name="query_product",
    )(far(tokens), weight)


def image_product(d_queries, weight, held, row0, total):
    rows, depth = d_queries.shape
    width = weight.shape[0]
    step = 256
    steps = rows // step

    def body(x_ref, w_ref, *refs):
        o_ref, buf, sem = refs[-3:]

        def put(i):
            return pltpu.make_async_copy(
                buf.at[i], o_ref.at[pl.ds(row0 + i * step, step), :], sem.at[i]
            )

        for i in range(steps):
            buf[i] = dot(x_ref[i * step : (i + 1) * step, :], w_ref[...], NT).astype(BF16)
            put(i).start()
        for i in range(steps):
            put(i).wait()

    more = [] if held is None else [held]
    return pl.pallas_call(
        body,
        in_specs=[VMEM, VMEM] + [ANY] * len(more),
        out_specs=ANY,
        out_shape=shape_of(total, width),
        scratch_shapes=[pltpu.VMEM((steps, step, width), BF16), pltpu.SemaphoreType.DMA((steps,))],
        input_output_aliases={2: 0} if more else {},
        compiler_params=params(24),
        cost_estimate=cost(2 * rows * depth * width, 2 * (rows * depth + depth * width)),
        name="image_product",
    )(d_queries, weight, *more)


def select(ids, prompt_of, same, other, dims):
    samp_dev, n_grp, n_dev, halves = dims
    _, block_len, width = same.shape
    part = samp_dev // halves

    def body(ids_ref, prompt_ref, same_ref, other_ref, *outs):
        for k in range(n_grp):
            base = ((ids_ref[0] ^ k) * n_dev + ids_ref[1]) * samp_dev
            for s in range(samp_dev):
                rel = prompt_ref[base + s] ^ ids_ref[1]
                out = outs[k * halves + s // part]

                @pl.when(rel & 1 == 0)
                def _():
                    out[s % part] = same_ref[rel >> 1]

                @pl.when(rel & 1 == 1)
                def _():
                    out[s % part] = other_ref[rel >> 1]

    return pl.pallas_call(
        body,
        in_specs=[SMEM, SMEM, VMEM, VMEM],
        out_specs=[VMEM] * (n_grp * halves),
        out_shape=[shape_of(part, block_len, width)] * (n_grp * halves),
        compiler_params=params(16),
        name="select",
    )(ids, prompt_of, same, other)


def attend(ids, prompt_of, lens, queries, grads, slots, held, first, dims):
    samp_dev, img_len, inner, n_grp, n_dev = dims
    part, block_len, _ = slots[0].shape
    full_len = n_grp * block_len
    scale = 1.0 / math.sqrt(HD)

    def body(ids_ref, prompt_ref, len_ref, q_ref, g_ref, *refs):
        ins = refs[:n_grp]
        dq_ref, ctx_ref = refs[-(n_grp + 4)], refs[-(n_grp + 3)]
        outs = refs[-(n_grp + 2) : -2]
        buf, sem = refs[-2:]
        row = lax.broadcasted_iota(jnp.int32, (full_len, 1), 0)
        token = ((row // block_len) ^ ids_ref[0]) * block_len + row % block_len
        zero = jnp.zeros((full_len, HD), BF16)
        base = (ids_ref[0] * n_dev + ids_ref[1]) * samp_dev + first

        def put(s):
            return pltpu.make_async_copy(
                buf.at[s], ctx_ref.at[pl.ds((first + s) * img_len, img_len), :], sem.at[s]
            )

        def sample(s):
            at = slice(s * img_len, (s + 1) * img_len)
            all_at = slice((first + s) * img_len, (first + s + 1) * img_len)
            live = (token < len_ref[prompt_ref[base + s]])[None]
            kv = jnp.concatenate([r[s] for r in ins], axis=0)
            for h in range(0, HEADS, 2):
                one = slice(h * HD, (h + 1) * HD)
                two = slice((h + 1) * HD, (h + 2) * HD)
                pair = slice(h * HD, (h + 2) * HD)
                v_one = slice(inner + h * HD, inner + (h + 1) * HD)
                v_two = slice(inner + (h + 1) * HD, inner + (h + 2) * HD)
                k1, k2, v1, v2 = kv[:, one], kv[:, two], kv[:, v_one], kv[:, v_two]
                keys = jnp.concatenate(
                    [jnp.concatenate([k1, zero], 1), jnp.concatenate([zero, k2], 1)], 0
                )
                values = jnp.concatenate(
                    [jnp.concatenate([v1, zero], 1), jnp.concatenate([zero, v2], 1)], 0
                )
                scores = jnp.stack([dot(k1, q_ref[at, one], NT), dot(k2, q_ref[at, two], NT)])
                d_soft = jnp.stack(
                    [dot(v1, g_ref[all_at, one], NT), dot(v2, g_ref[all_at, two], NT)]
                )
                scores = jnp.where(live, scores * scale, NEG_FILL)
                expd = jnp.exp(scores - jnp.max(scores, axis=1, keepdims=True))
                soft = expd * (1.0 / jnp.sum(expd, axis=1, keepdims=True))
                soft_b = soft.astype(BF16).reshape(2 * full_len, img_len)
                mean = jnp.sum(d_soft * soft, axis=1, keepdims=True)
                d_scores = (
                    (soft * (d_soft - mean) * scale).astype(BF16).reshape(2 * full_len, img_len)
                )
                buf[s, :, pair] = dot(soft_b, values, TN).astype(BF16)
                dq_ref[at, pair] = dot(d_scores, keys, TN).astype(BF16)
                d_keys = dot(d_scores, q_ref[at, pair], NN).astype(BF16)
                d_values = dot(soft_b, g_ref[all_at, pair], NN).astype(BF16)
                for k in range(n_grp):
                    a = slice(k * block_len, (k + 1) * block_len)
                    b = slice(full_len + k * block_len, full_len + (k + 1) * block_len)
                    outs[k][s, :, one] = d_keys[a, :HD]
                    outs[k][s, :, two] = d_keys[b, HD:]
                    outs[k][s, :, v_one] = d_values[a, :HD]
                    outs[k][s, :, v_two] = d_values[b, HD:]
            put(s).start()

        for s in range(part):
            sample(s)
        for s in range(part):
            put(s).wait()

    more = [] if held is None else [held]
    rows = part * img_len
    return pl.pallas_call(
        body,
        in_specs=[SMEM, SMEM, SMEM, VMEM, VMEM] + [VMEM] * n_grp + [ANY] * len(more),
        out_specs=[VMEM, ANY] + [VMEM] * n_grp,
        out_shape=[shape_of(rows, inner), shape_of(samp_dev * img_len, inner)]
        + [shape_of(part, block_len, 2 * inner)] * n_grp,
        scratch_shapes=[pltpu.VMEM((part, img_len, inner), BF16), pltpu.SemaphoreType.DMA((part,))],
        input_output_aliases={5 + n_grp: 1} if more else {},
        compiler_params=params(24),
        cost_estimate=cost(20 * rows * full_len * inner, 8 * rows * inner),
        name="attend",
    )(ids, prompt_of, lens, queries, grads, *slots, *more)


def combine(ids, prompt_of, arrived, dims):
    samp_dev, n_grp, n_dev, halves = dims
    part, block_len, width = arrived[0][0].shape
    chips = n_dev // 2

    def body(ids_ref, prompt_ref, *refs):
        same_ref, other_ref, acc_ref = refs[-3:]
        acc_ref[...] = jnp.zeros_like(acc_ref)
        for k in range(n_grp):
            base = ((ids_ref[0] ^ k) * n_dev + ids_ref[1]) * samp_dev
            for s in range(samp_dev):
                rel = prompt_ref[base + s] ^ ids_ref[1]
                slot = (rel & 1) * chips + (rel >> 1)
                acc_ref[slot] += refs[k * halves + s // part][s % part].astype(F32)
        same_ref[...] = acc_ref[:chips]
        other_ref[...] = acc_ref[chips:].astype(BF16)

    return pl.pallas_call(
        body,
        in_specs=[SMEM, SMEM] + [VMEM] * (n_grp * halves),
        out_specs=[VMEM, VMEM],
        out_shape=[
            shape_of(chips, block_len, width, dtype=F32),
            shape_of(chips, block_len, width),
        ],
        scratch_shapes=[pltpu.VMEM((2 * chips, block_len, width), F32)],
        compiler_params=params(16),
        name="combine",
    )(ids, prompt_of, *[x for pair in arrived for x in pair])


def shards(captions, kv_weight, image_tokens, q_weight, context_grad, sample_prompt, caption_len):
    n_grp = lax.axis_size("grp")
    n_dev = lax.axis_size("dev")
    grp_at = lax.axis_index("grp")
    dev_at = lax.axis_index("dev")
    samp_dev, img_len, width_img = image_tokens.shape
    _, block_len, width_cap = captions.shape
    inner = q_weight.shape[1]
    share = width_cap // n_grp
    chips = n_dev // 2
    part = samp_dev // HALVES
    rows = samp_dev * img_len
    ids = jnp.stack([grp_at, dev_at]).astype(jnp.int32)
    tokens = image_tokens.reshape(rows, width_img)
    grads = context_grad.reshape(rows, inner)

    def over_grp(blocks):
        return [blocks[0]] + [partner(blocks[k], "grp", n_grp, k) for k in range(1, n_grp)]

    whole = captions.reshape(block_len, width_cap)
    pieces = [lax.dynamic_slice_in_dim(whole, (grp_at ^ k) * share, share, 1) for k in range(n_grp)]
    (kv_near,) = fetch([kv_weight])
    partial = project(over_grp(pieces), kv_near, NN, 2 * inner)
    queries = []
    for half in range(HALVES):
        queries.append(
            query_product(tokens, q_weight, half * part * img_len, part * img_len)
        )
    *queries, grads = fetch(queries + [grads])
    summed = over_grp(partial)
    kv_block = sum(summed[1:], summed[0]).astype(BF16)

    same = jnp.stack([kv_block] + [partner(kv_block, "dev", n_dev, 2 * k) for k in range(1, chips)])
    other = partner(same, "dev", n_dev, 1)
    dims = (samp_dev, n_grp, n_dev, HALVES)
    chosen = select(ids, sample_prompt, same, other, dims)
    slots = [over_grp(chosen[half::HALVES]) for half in range(HALVES)]

    context, arrived, d_queries = None, [], []
    for half in range(HALVES):
        d_q, context, *d_kv = attend(
            ids,
            sample_prompt,
            caption_len,
            queries[half],
            grads,
            slots[half],
            context,
            half * part,
            (samp_dev, img_len, inner, n_grp, n_dev),
        )
        d_queries.append(d_q)
        arrived.append(over_grp(d_kv))

    image_grad = None
    for half in range(HALVES):
        image_grad = image_product(
            d_queries[half], q_weight, image_grad, half * part * img_len, rows
        )

    mine, theirs = combine(ids, sample_prompt, list(zip(*arrived)), dims)
    both = mine + partner(theirs, "dev", n_dev, 1).astype(F32)
    kv_grad = both[0]
    for k in range(1, chips):
        sent = partner(both[k].astype(BF16), "dev", n_dev, 2 * k)
        kv_grad = kv_grad + sent.astype(F32)
    grad_blocks = over_grp([kv_grad.astype(BF16)] * n_grp)
    shares = over_grp(project(grad_blocks, kv_weight, NT, share))
    caption_grad = jnp.zeros((block_len, width_cap), F32)
    for k in range(n_grp):
        caption_grad = lax.dynamic_update_slice_in_dim(
            caption_grad, shares[k], (grp_at ^ k) * share, 1
        )
    return (
        context.reshape(samp_dev, img_len, inner),
        image_grad.reshape(samp_dev, img_len, width_img),
        caption_grad[None],
    )


def solution(mesh):
    placed = (
        P("dev", "grp", None),
        P("grp", None),
        P(("grp", "dev"), None, None),
        P(),
        P(("grp", "dev"), None, None),
        P(),
        P(),
    )

    return jax.shard_map(
        shards,
        mesh=mesh,
        in_specs=placed,
        out_specs=(
            P(("grp", "dev"), None, None),
            P(("grp", "dev"), None, None),
            P("dev", "grp", None),
        ),
        check_vma=False,
    )
```

```python
import math

import jax
import jax.numpy as jnp
from jax import lax
from jax.experimental import pallas as pl
from jax.experimental.pallas import tpu as pltpu
from jax.sharding import PartitionSpec as P

HEADS = 8
HD = 128
NEG_FILL = -1e30
HALVES = 2
F32 = jnp.float32
BF16 = jnp.bfloat16
MIB = 1 << 20
NN = (((1,), (0,)), ((), ()))
NT = (((1,), (1,)), ((), ()))
TN = (((0,), (0,)), ((), ()))
VMEM = pl.BlockSpec(memory_space=pltpu.VMEM)
SMEM = pl.BlockSpec(memory_space=pltpu.SMEM)
ANY = pl.BlockSpec(memory_space=pl.ANY)
HBM = pl.BlockSpec(memory_space=pltpu.HBM)


def dot(a, b, dims):
    return lax.dot_general(a, b, dims, preferred_element_type=F32)


def partner(x, axis, size, k):
    return lax.ppermute(x, axis, [(i, i ^ k) for i in range(size)])


def shape_of(*dims, dtype=BF16):
    return jax.ShapeDtypeStruct(dims, dtype)


def params(limit):
    return pltpu.CompilerParams(vmem_limit_bytes=limit * MIB)


def cost(flops, size):
    return pl.CostEstimate(flops=flops, bytes_accessed=size, transcendentals=0)


def project(blocks, weight, dims, width):
    n = len(blocks)
    rows = blocks[0].shape[0]
    step = min(width, 512)

    def body(*refs):
        w_ref = refs[n]
        left = jnp.concatenate([r[...] for r in refs[:n]], axis=0)
        for start in range(0, width, step):
            cols = slice(start, start + step)
            w = w_ref[:, cols] if dims is NN else w_ref[cols, :]
            out = dot(left, w, dims)
            for k in range(n):
                refs[n + 1 + k][:, cols] = out[k * rows : (k + 1) * rows]

    return pl.pallas_call(
        body,
        in_specs=[VMEM] * (n + 1),
        out_specs=[VMEM] * n,
        out_shape=[shape_of(rows, width, dtype=F32)] * n,
        compiler_params=params(16),
        cost_estimate=cost(2 * n * rows * weight.size, weight.size * 2),
        name="project",
    )(*blocks, weight)


def far(x):
    return pltpu.with_memory_space_constraint(x, pltpu.HBM)


def fetch(arrays):
    n = len(arrays)

    def body(*refs):
        sem = refs[-1]
        copies = [pltpu.make_async_copy(refs[i], refs[n + i], sem.at[i]) for i in range(n)]
        for c in copies:
            c.start()
        for c in copies:
            c.wait()

    return pl.pallas_call(
        body,
        in_specs=[HBM] * n,
        out_specs=[VMEM] * n,
        out_shape=[shape_of(*a.shape) for a in arrays],
        scratch_shapes=[pltpu.SemaphoreType.DMA((n,))],
        compiler_params=params(16),
        cost_estimate=cost(0, sum(a.size for a in arrays) * 4),
        name="fetch",
    )(*[far(a) for a in arrays])


def query_product(tokens, weight, row0, rows):
    depth, width = weight.shape
    step = 256
    steps = rows // step

    def body(x_ref, w_ref, o_ref, x_buf, o_buf, x_sem, o_sem):
        def get(i):
            at = pl.ds(row0 + i * step, step)
            return pltpu.make_async_copy(x_ref.at[at, :], x_buf.at[i], x_sem.at[i])

        def put(i):
            at = pl.ds(i * step, step)
            return pltpu.make_async_copy(o_buf.at[i], o_ref.at[at, :], o_sem.at[i])

        for i in range(steps):
            get(i).start()
        for i in range(steps):
            get(i).wait()
            o_buf[i] = dot(x_buf[i], w_ref[...], NN).astype(BF16)
            put(i).start()
        for i in range(steps):
            put(i).wait()

    return pl.pallas_call(
        body,
        in_specs=[HBM, VMEM],
        out_specs=HBM,
        out_shape=pltpu.HBM((rows, width), BF16),
        scratch_shapes=[
            pltpu.VMEM((steps, step, depth), BF16),
            pltpu.VMEM((steps, step, width), BF16),
            pltpu.SemaphoreType.DMA((steps,)),
            pltpu.SemaphoreType.DMA((steps,)),
        ],
        compiler_params=params(24),
        cost_estimate=cost(2 * rows * depth * width, 2 * (rows * depth + depth * width)),
        name="query_product",
    )(far(tokens), weight)


def image_product(d_queries, weight, held, row0, total):
    rows, depth = d_queries.shape
    width = weight.shape[0]
    step = 256
    steps = rows // step

    def body(x_ref, w_ref, *refs):
        o_ref, buf, sem = refs[-3:]

        def put(i):
            return pltpu.make_async_copy(
                buf.at[i], o_ref.at[pl.ds(row0 + i * step, step), :], sem.at[i]
            )

        for i in range(steps):
            buf[i] = dot(x_ref[i * step : (i + 1) * step, :], w_ref[...], NT).astype(BF16)
            put(i).start()
        for i in range(steps):
            put(i).wait()

    more = [] if held is None else [held]
    return pl.pallas_call(
        body,
        in_specs=[VMEM, VMEM] + [ANY] * len(more),
        out_specs=ANY,
        out_shape=shape_of(total, width),
        scratch_shapes=[pltpu.VMEM((steps, step, width), BF16), pltpu.SemaphoreType.DMA((steps,))],
        input_output_aliases={2: 0} if more else {},
        compiler_params=params(24),
        cost_estimate=cost(2 * rows * depth * width, 2 * (rows * depth + depth * width)),
        name="image_product",
    )(d_queries, weight, *more)


def select(ids, prompt_of, same, other, dims):
    samp_dev, n_grp, n_dev, halves = dims
    _, block_len, width = same.shape
    part = samp_dev // halves

    def body(ids_ref, prompt_ref, same_ref, other_ref, *outs):
        for k in range(n_grp):
            base = ((ids_ref[0] ^ k) * n_dev + ids_ref[1]) * samp_dev
            for s in range(samp_dev):
                rel = prompt_ref[base + s] ^ ids_ref[1]
                out = outs[k * halves + s // part]

                @pl.when(rel & 1 == 0)
                def _():
                    out[s % part] = same_ref[rel >> 1]

                @pl.when(rel & 1 == 1)
                def _():
                    out[s % part] = other_ref[rel >> 1]

    return pl.pallas_call(
        body,
        in_specs=[SMEM, SMEM, VMEM, VMEM],
        out_specs=[VMEM] * (n_grp * halves),
        out_shape=[shape_of(part, block_len, width)] * (n_grp * halves),
        compiler_params=params(16),
        name="select",
    )(ids, prompt_of, same, other)


def attend(ids, prompt_of, lens, queries, grads, slots, held, first, dims):
    samp_dev, img_len, inner, n_grp, n_dev = dims
    part, block_len, _ = slots[0].shape
    full_len = n_grp * block_len
    scale = 1.0 / math.sqrt(HD)

    def body(ids_ref, prompt_ref, len_ref, q_ref, g_ref, *refs):
        ins = refs[:n_grp]
        dq_ref, ctx_ref = refs[-(n_grp + 4)], refs[-(n_grp + 3)]
        outs = refs[-(n_grp + 2) : -2]
        buf, sem = refs[-2:]
        row = lax.broadcasted_iota(jnp.int32, (full_len, 1), 0)
        token = ((row // block_len) ^ ids_ref[0]) * block_len + row % block_len
        zero = jnp.zeros((full_len, HD), BF16)
        base = (ids_ref[0] * n_dev + ids_ref[1]) * samp_dev + first

        def put(s):
            return pltpu.make_async_copy(
                buf.at[s], ctx_ref.at[pl.ds((first + s) * img_len, img_len), :], sem.at[s]
            )

        items = [(s, h) for s in range(part) for h in range(0, HEADS, 2)]
        kept = {}

        def columns(h):
            one = slice(h * HD, (h + 1) * HD)
            two = slice((h + 1) * HD, (h + 2) * HD)
            pair = slice(h * HD, (h + 2) * HD)
            v_one = slice(inner + h * HD, inner + (h + 1) * HD)
            v_two = slice(inner + (h + 1) * HD, inner + (h + 2) * HD)
            return one, two, pair, v_one, v_two

        def rows_of(s):
            at = slice(s * img_len, (s + 1) * img_len)
            return at, slice((first + s) * img_len, (first + s + 1) * img_len)

        def block(s, cols):
            return jnp.concatenate([r[s, :, cols] for r in ins], axis=0)

        def diagonal(s, one, two):
            a, b = block(s, one), block(s, two)
            return jnp.concatenate(
                [jnp.concatenate([a, zero], 1), jnp.concatenate([zero, b], 1)], 0
            )

        def enter(n):
            s, h = items[n]
            at, all_at = rows_of(s)
            one, two, pair, v_one, v_two = columns(h)
            size = (2, full_len, img_len)
            scores = dot(diagonal(s, one, two), q_ref[at, pair], NT).reshape(size)
            d_soft = dot(diagonal(s, v_one, v_two), g_ref[all_at, pair], NT).reshape(size)
            kept[n] = scores, d_soft

        def weigh(n):
            s, _ = items[n]
            scores, d_soft = kept[n]
            live = (token < len_ref[prompt_ref[base + s]])[None]
            scores = jnp.where(live, scores * scale, NEG_FILL)
            expd = jnp.exp(scores - jnp.max(scores, axis=1, keepdims=True))
            soft = expd * (1.0 / jnp.sum(expd, axis=1, keepdims=True))
            mean = jnp.sum(d_soft * soft, axis=1, keepdims=True)
            d_scores = (soft * (d_soft - mean) * scale).astype(BF16)
            size = (2 * full_len, img_len)
            kept[n] = soft.astype(BF16).reshape(size), d_scores.reshape(size)

        def leave(n):
            s, h = items[n]
            at, all_at = rows_of(s)
            one, two, pair, v_one, v_two = columns(h)
            soft_b, d_scores = kept.pop(n)
            d_keys = dot(d_scores, q_ref[at, pair], NN).astype(BF16)
            d_values = dot(soft_b, g_ref[all_at, pair], NN).astype(BF16)
            buf[s, :, pair] = dot(soft_b, diagonal(s, v_one, v_two), TN).astype(BF16)
            dq_ref[at, pair] = dot(d_scores, diagonal(s, one, two), TN).astype(BF16)
            for k in range(n_grp):
                a = slice(k * block_len, (k + 1) * block_len)
                b = slice(full_len + k * block_len, full_len + (k + 1) * block_len)
                outs[k][s, :, one] = d_keys[a, :HD]
                outs[k][s, :, two] = d_keys[b, HD:]
                outs[k][s, :, v_one] = d_values[a, :HD]
                outs[k][s, :, v_two] = d_values[b, HD:]
            if h == HEADS - 2:
                put(s).start()

        enter(0)
        for n in range(len(items)):
            if n + 1 < len(items):
                enter(n + 1)
            weigh(n)
            leave(n)
        for s in range(part):
            put(s).wait()

    more = [] if held is None else [held]
    rows = part * img_len
    return pl.pallas_call(
        body,
        in_specs=[SMEM, SMEM, SMEM, VMEM, VMEM] + [VMEM] * n_grp + [ANY] * len(more),
        out_specs=[VMEM, ANY] + [VMEM] * n_grp,
        out_shape=[shape_of(rows, inner), shape_of(samp_dev * img_len, inner)]
        + [shape_of(part, block_len, 2 * inner)] * n_grp,
        scratch_shapes=[pltpu.VMEM((part, img_len, inner), BF16), pltpu.SemaphoreType.DMA((part,))],
        input_output_aliases={5 + n_grp: 1} if more else {},
        compiler_params=params(24),
        cost_estimate=cost(20 * rows * full_len * inner, 8 * rows * inner),
        name="attend",
    )(ids, prompt_of, lens, queries, grads, *slots, *more)


def combine(ids, prompt_of, arrived, dims):
    samp_dev, n_grp, n_dev, halves = dims
    part, block_len, width = arrived[0][0].shape
    chips = n_dev // 2

    def body(ids_ref, prompt_ref, *refs):
        same_ref, other_ref, acc_ref = refs[-3:]
        acc_ref[...] = jnp.zeros_like(acc_ref)
        for k in range(n_grp):
            base = ((ids_ref[0] ^ k) * n_dev + ids_ref[1]) * samp_dev
            for s in range(samp_dev):
                rel = prompt_ref[base + s] ^ ids_ref[1]
                slot = (rel & 1) * chips + (rel >> 1)
                acc_ref[slot] += refs[k * halves + s // part][s % part].astype(F32)
        same_ref[...] = acc_ref[:chips]
        other_ref[...] = acc_ref[chips:].astype(BF16)

    return pl.pallas_call(
        body,
        in_specs=[SMEM, SMEM] + [VMEM] * (n_grp * halves),
        out_specs=[VMEM, VMEM],
        out_shape=[
            shape_of(chips, block_len, width, dtype=F32),
            shape_of(chips, block_len, width),
        ],
        scratch_shapes=[pltpu.VMEM((2 * chips, block_len, width), F32)],
        compiler_params=params(16),
        name="combine",
    )(ids, prompt_of, *[x for pair in arrived for x in pair])


def shards(captions, kv_weight, image_tokens, q_weight, context_grad, sample_prompt, caption_len):
    n_grp = lax.axis_size("grp")
    n_dev = lax.axis_size("dev")
    grp_at = lax.axis_index("grp")
    dev_at = lax.axis_index("dev")
    samp_dev, img_len, width_img = image_tokens.shape
    _, block_len, width_cap = captions.shape
    inner = q_weight.shape[1]
    share = width_cap // n_grp
    chips = n_dev // 2
    part = samp_dev // HALVES
    rows = samp_dev * img_len
    ids = jnp.stack([grp_at, dev_at]).astype(jnp.int32)
    tokens = image_tokens.reshape(rows, width_img)
    grads = context_grad.reshape(rows, inner)

    def over_grp(blocks):
        return [blocks[0]] + [partner(blocks[k], "grp", n_grp, k) for k in range(1, n_grp)]

    whole = captions.reshape(block_len, width_cap)
    pieces = [lax.dynamic_slice_in_dim(whole, (grp_at ^ k) * share, share, 1) for k in range(n_grp)]
    (kv_near,) = fetch([kv_weight])
    partial = project(over_grp(pieces), kv_near, NN, 2 * inner)
    queries = []
    for half in range(HALVES):
        queries.append(
            query_product(tokens, q_weight, half * part * img_len, part * img_len)
        )
    *queries, grads = fetch(queries + [grads])
    summed = over_grp(partial)
    kv_block = sum(summed[1:], summed[0]).astype(BF16)

    same = jnp.stack([kv_block] + [partner(kv_block, "dev", n_dev, 2 * k) for k in range(1, chips)])
    other = partner(same, "dev", n_dev, 1)
    dims = (samp_dev, n_grp, n_dev, HALVES)
    chosen = select(ids, sample_prompt, same, other, dims)
    slots = [over_grp(chosen[half::HALVES]) for half in range(HALVES)]

    context, arrived, d_queries = None, [], []
    for half in range(HALVES):
        d_q, context, *d_kv = attend(
            ids,
            sample_prompt,
            caption_len,
            queries[half],
            grads,
            slots[half],
            context,
            half * part,
            (samp_dev, img_len, inner, n_grp, n_dev),
        )
        d_queries.append(d_q)
        arrived.append(over_grp(d_kv))

    image_grad = None
    for half in range(HALVES):
        image_grad = image_product(
            d_queries[half], q_weight, image_grad, half * part * img_len, rows
        )

    mine, theirs = combine(ids, sample_prompt, list(zip(*arrived)), dims)
    both = mine + partner(theirs, "dev", n_dev, 1).astype(F32)
    kv_grad = both[0]
    for k in range(1, chips):
        sent = partner(both[k].astype(BF16), "dev", n_dev, 2 * k)
        kv_grad = kv_grad + sent.astype(F32)
    grad_blocks = over_grp([kv_grad.astype(BF16)] * n_grp)
    shares = over_grp(project(grad_blocks, kv_weight, NT, share))
    caption_grad = jnp.zeros((block_len, width_cap), F32)
    for k in range(n_grp):
        caption_grad = lax.dynamic_update_slice_in_dim(
            caption_grad, shares[k], (grp_at ^ k) * share, 1
        )
    return (
        context.reshape(samp_dev, img_len, inner),
        image_grad.reshape(samp_dev, img_len, width_img),
        caption_grad[None],
    )


def solution(mesh):
    placed = (
        P("dev", "grp", None),
        P("grp", None),
        P(("grp", "dev"), None, None),
        P(),
        P(("grp", "dev"), None, None),
        P(),
        P(),
    )

    return jax.shard_map(
        shards,
        mesh=mesh,
        in_specs=placed,
        out_specs=(
            P(("grp", "dev"), None, None),
            P(("grp", "dev"), None, None),
            P("dev", "grp", None),
        ),
        check_vma=False,
    )
```

```python
import math

import jax
import jax.numpy as jnp
from jax import lax
from jax.experimental import pallas as pl
from jax.experimental.pallas import tpu as pltpu
from jax.sharding import PartitionSpec as P

HEADS = 8
HD = 128
NEG_FILL = -1e30
HALVES = 2
F32 = jnp.float32
BF16 = jnp.bfloat16
MIB = 1 << 20
NN = (((1,), (0,)), ((), ()))
NT = (((1,), (1,)), ((), ()))
TN = (((0,), (0,)), ((), ()))
VMEM = pl.BlockSpec(memory_space=pltpu.VMEM)
SMEM = pl.BlockSpec(memory_space=pltpu.SMEM)
ANY = pl.BlockSpec(memory_space=pl.ANY)
HBM = pl.BlockSpec(memory_space=pltpu.HBM)


def dot(a, b, dims):
    return lax.dot_general(a, b, dims, preferred_element_type=F32)


def partner(x, axis, size, k):
    return lax.ppermute(x, axis, [(i, i ^ k) for i in range(size)])


def shape_of(*dims, dtype=BF16):
    return jax.ShapeDtypeStruct(dims, dtype)


def params(limit):
    return pltpu.CompilerParams(vmem_limit_bytes=limit * MIB)


def cost(flops, size):
    return pl.CostEstimate(flops=flops, bytes_accessed=size, transcendentals=0)


def project(blocks, weight, dims, width):
    n = len(blocks)
    rows = blocks[0].shape[0]
    step = min(width, 512)

    def body(*refs):
        w_ref = refs[n]
        left = jnp.concatenate([r[...] for r in refs[:n]], axis=0)
        for start in range(0, width, step):
            cols = slice(start, start + step)
            w = w_ref[:, cols] if dims is NN else w_ref[cols, :]
            out = dot(left, w, dims)
            for k in range(n):
                refs[n + 1 + k][:, cols] = out[k * rows : (k + 1) * rows]

    return pl.pallas_call(
        body,
        in_specs=[VMEM] * (n + 1),
        out_specs=[VMEM] * n,
        out_shape=[shape_of(rows, width, dtype=F32)] * n,
        compiler_params=params(16),
        cost_estimate=cost(2 * n * rows * weight.size, weight.size * 2),
        name="project",
    )(*blocks, weight)


def far(x):
    return pltpu.with_memory_space_constraint(x, pltpu.HBM)


def fetch(arrays):
    n = len(arrays)

    def body(*refs):
        sem = refs[-1]
        copies = [pltpu.make_async_copy(refs[i], refs[n + i], sem.at[i]) for i in range(n)]
        for c in copies:
            c.start()
        for c in copies:
            c.wait()

    return pl.pallas_call(
        body,
        in_specs=[HBM] * n,
        out_specs=[VMEM] * n,
        out_shape=[shape_of(*a.shape) for a in arrays],
        scratch_shapes=[pltpu.SemaphoreType.DMA((n,))],
        compiler_params=params(16),
        cost_estimate=cost(0, sum(a.size for a in arrays) * 4),
        name="fetch",
    )(*[far(a) for a in arrays])


def query_product(tokens, weight, row0, rows):
    depth, width = weight.shape
    step = 256
    steps = rows // step

    def body(x_ref, w_ref, o_ref, x_buf, o_buf, x_sem, o_sem):
        def get(i):
            at = pl.ds(row0 + i * step, step)
            return pltpu.make_async_copy(x_ref.at[at, :], x_buf.at[i], x_sem.at[i])

        def put(i):
            at = pl.ds(i * step, step)
            return pltpu.make_async_copy(o_buf.at[i], o_ref.at[at, :], o_sem.at[i])

        for i in range(steps):
            get(i).start()
        for i in range(steps):
            get(i).wait()
            o_buf[i] = dot(x_buf[i], w_ref[...], NN).astype(BF16)
            put(i).start()
        for i in range(steps):
            put(i).wait()

    return pl.pallas_call(
        body,
        in_specs=[HBM, VMEM],
        out_specs=HBM,
        out_shape=pltpu.HBM((rows, width), BF16),
        scratch_shapes=[
            pltpu.VMEM((steps, step, depth), BF16),
            pltpu.VMEM((steps, step, width), BF16),
            pltpu.SemaphoreType.DMA((steps,)),
            pltpu.SemaphoreType.DMA((steps,)),
        ],
        compiler_params=params(24),
        cost_estimate=cost(2 * rows * depth * width, 2 * (rows * depth + depth * width)),
        name="query_product",
    )(far(tokens), weight)


def image_product(d_queries, weight, context, held, row0, total):
    rows, depth = d_queries.shape
    width = weight.shape[0]
    step = 256
    steps = rows // step

    def body(x_ref, w_ref, c_ref, *refs):
        o_ref, all_ref, buf, sem, c_sem = refs[-5:]
        moved = pltpu.make_async_copy(c_ref, all_ref.at[pl.ds(row0, rows), :], c_sem)
        moved.start()

        def put(i):
            return pltpu.make_async_copy(
                buf.at[i], o_ref.at[pl.ds(row0 + i * step, step), :], sem.at[i]
            )

        for i in range(steps):
            buf[i] = dot(x_ref[i * step : (i + 1) * step, :], w_ref[...], NT).astype(BF16)
            put(i).start()
        for i in range(steps):
            put(i).wait()
        moved.wait()

    more = [] if held is None else list(held)
    return pl.pallas_call(
        body,
        in_specs=[VMEM, VMEM, VMEM] + [ANY] * len(more),
        out_specs=[ANY, ANY],
        out_shape=[shape_of(total, width), shape_of(total, depth)],
        scratch_shapes=[
            pltpu.VMEM((steps, step, width), BF16),
            pltpu.SemaphoreType.DMA((steps,)),
            pltpu.SemaphoreType.DMA,
        ],
        input_output_aliases={3: 0, 4: 1} if more else {},
        compiler_params=params(24),
        cost_estimate=cost(2 * rows * depth * width, 2 * (rows * depth + depth * width)),
        name="image_product",
    )(d_queries, weight, context, *more)


def select(ids, prompt_of, same, other, half, dims):
    samp_dev, n_grp, n_dev, halves = dims
    _, block_len, width = same.shape
    part = samp_dev // halves

    def body(ids_ref, prompt_ref, same_ref, other_ref, *outs):
        for k in range(n_grp):
            base = ((ids_ref[0] ^ k) * n_dev + ids_ref[1]) * samp_dev
            for s in range(part):
                rel = prompt_ref[base + half * part + s] ^ ids_ref[1]

                @pl.when(rel & 1 == 0)
                def _():
                    outs[k][s] = same_ref[rel >> 1]

                @pl.when(rel & 1 == 1)
                def _():
                    outs[k][s] = other_ref[rel >> 1]

    return pl.pallas_call(
        body,
        in_specs=[SMEM, SMEM, VMEM, VMEM],
        out_specs=[VMEM] * n_grp,
        out_shape=[shape_of(part, block_len, width)] * n_grp,
        compiler_params=params(16),
        name="select",
    )(ids, prompt_of, same, other)


def attend(ids, prompt_of, lens, queries, grads, slots, first, dims):
    samp_dev, img_len, inner, n_grp, n_dev = dims
    part, block_len, _ = slots[0].shape
    full_len = n_grp * block_len
    scale = 1.0 / math.sqrt(HD)

    def body(ids_ref, prompt_ref, len_ref, q_ref, g_ref, *refs):
        ins = refs[:n_grp]
        dq_ref, ctx_ref, *outs = refs[n_grp:]
        row = lax.broadcasted_iota(jnp.int32, (full_len, 1), 0)
        token = ((row // block_len) ^ ids_ref[0]) * block_len + row % block_len
        zero = jnp.zeros((full_len, HD), BF16)
        base = (ids_ref[0] * n_dev + ids_ref[1]) * samp_dev + first

        items = [(s, h) for s in range(part) for h in range(0, HEADS, 2)]
        kept = {}

        def columns(h):
            one = slice(h * HD, (h + 1) * HD)
            two = slice((h + 1) * HD, (h + 2) * HD)
            pair = slice(h * HD, (h + 2) * HD)
            v_one = slice(inner + h * HD, inner + (h + 1) * HD)
            v_two = slice(inner + (h + 1) * HD, inner + (h + 2) * HD)
            return one, two, pair, v_one, v_two

        def rows_of(s):
            at = slice(s * img_len, (s + 1) * img_len)
            return at, slice((first + s) * img_len, (first + s + 1) * img_len)

        def block(s, cols):
            return jnp.concatenate([r[s, :, cols] for r in ins], axis=0)

        def diagonal(s, one, two):
            a, b = block(s, one), block(s, two)
            return jnp.concatenate(
                [jnp.concatenate([a, zero], 1), jnp.concatenate([zero, b], 1)], 0
            )

        def enter(n):
            s, h = items[n]
            at, all_at = rows_of(s)
            one, two, pair, v_one, v_two = columns(h)
            size = (2, full_len, img_len)
            scores = dot(diagonal(s, one, two), q_ref[at, pair], NT).reshape(size)
            d_soft = dot(diagonal(s, v_one, v_two), g_ref[all_at, pair], NT).reshape(size)
            kept[n] = scores, d_soft

        def weigh(n):
            s, _ = items[n]
            scores, d_soft = kept[n]
            live = (token < len_ref[prompt_ref[base + s]])[None]
            scores = jnp.where(live, scores * scale, NEG_FILL)
            expd = jnp.exp(scores - jnp.max(scores, axis=1, keepdims=True))
            soft = expd * (1.0 / jnp.sum(expd, axis=1, keepdims=True))
            mean = jnp.sum(d_soft * soft, axis=1, keepdims=True)
            d_scores = (soft * (d_soft - mean) * scale).astype(BF16)
            size = (2 * full_len, img_len)
            kept[n] = soft.astype(BF16).reshape(size), d_scores.reshape(size)

        def leave(n):
            s, h = items[n]
            at, all_at = rows_of(s)
            one, two, pair, v_one, v_two = columns(h)
            soft_b, d_scores = kept.pop(n)
            d_keys = dot(d_scores, q_ref[at, pair], NN).astype(BF16)
            d_values = dot(soft_b, g_ref[all_at, pair], NN).astype(BF16)
            ctx_ref[at, pair] = dot(soft_b, diagonal(s, v_one, v_two), TN).astype(BF16)
            dq_ref[at, pair] = dot(d_scores, diagonal(s, one, two), TN).astype(BF16)
            for k in range(n_grp):
                a = slice(k * block_len, (k + 1) * block_len)
                b = slice(full_len + k * block_len, full_len + (k + 1) * block_len)
                outs[k][s, :, one] = d_keys[a, :HD]
                outs[k][s, :, two] = d_keys[b, HD:]
                outs[k][s, :, v_one] = d_values[a, :HD]
                outs[k][s, :, v_two] = d_values[b, HD:]

        enter(0)
        for n in range(len(items)):
            if n + 1 < len(items):
                enter(n + 1)
            weigh(n)
            leave(n)

    rows = part * img_len
    return pl.pallas_call(
        body,
        in_specs=[SMEM, SMEM, SMEM, VMEM, VMEM] + [VMEM] * n_grp,
        out_specs=[VMEM] * (n_grp + 2),
        out_shape=[shape_of(rows, inner)] * 2 + [shape_of(part, block_len, 2 * inner)] * n_grp,
        compiler_params=params(24),
        cost_estimate=cost(20 * rows * full_len * inner, 8 * rows * inner),
        name="attend",
    )(ids, prompt_of, lens, queries, grads, *slots)


def combine(ids, prompt_of, arrived, dims):
    samp_dev, n_grp, n_dev, halves = dims
    part, block_len, width = arrived[0][0].shape
    chips = n_dev // 2

    def body(ids_ref, prompt_ref, *refs):
        same_ref, other_ref, acc_ref = refs[-3:]
        acc_ref[...] = jnp.zeros_like(acc_ref)
        for k in range(n_grp):
            base = ((ids_ref[0] ^ k) * n_dev + ids_ref[1]) * samp_dev
            for s in range(samp_dev):
                rel = prompt_ref[base + s] ^ ids_ref[1]
                slot = (rel & 1) * chips + (rel >> 1)
                acc_ref[slot] += refs[k * halves + s // part][s % part].astype(F32)
        same_ref[...] = acc_ref[:chips]
        other_ref[...] = acc_ref[chips:].astype(BF16)

    return pl.pallas_call(
        body,
        in_specs=[SMEM, SMEM] + [VMEM] * (n_grp * halves),
        out_specs=[VMEM, VMEM],
        out_shape=[
            shape_of(chips, block_len, width, dtype=F32),
            shape_of(chips, block_len, width),
        ],
        scratch_shapes=[pltpu.VMEM((2 * chips, block_len, width), F32)],
        compiler_params=params(16),
        name="combine",
    )(ids, prompt_of, *[x for pair in arrived for x in pair])


def shards(captions, kv_weight, image_tokens, q_weight, context_grad, sample_prompt, caption_len):
    n_grp = lax.axis_size("grp")
    n_dev = lax.axis_size("dev")
    grp_at = lax.axis_index("grp")
    dev_at = lax.axis_index("dev")
    samp_dev, img_len, width_img = image_tokens.shape
    _, block_len, width_cap = captions.shape
    inner = q_weight.shape[1]
    share = width_cap // n_grp
    chips = n_dev // 2
    part = samp_dev // HALVES
    rows = samp_dev * img_len
    ids = jnp.stack([grp_at, dev_at]).astype(jnp.int32)
    tokens = image_tokens.reshape(rows, width_img)
    grads = context_grad.reshape(rows, inner)

    def over_grp(blocks):
        return [blocks[0]] + [partner(blocks[k], "grp", n_grp, k) for k in range(1, n_grp)]

    whole = captions.reshape(block_len, width_cap)
    pieces = [lax.dynamic_slice_in_dim(whole, (grp_at ^ k) * share, share, 1) for k in range(n_grp)]
    (kv_near,) = fetch([kv_weight])
    partial = project(over_grp(pieces), kv_near, NN, 2 * inner)
    queries = []
    for half in range(HALVES):
        queries.append(
            query_product(tokens, q_weight, half * part * img_len, part * img_len)
        )
    *queries, grads = fetch(queries + [grads])
    summed = over_grp(partial)
    kv_block = sum(summed[1:], summed[0]).astype(BF16)

    same = jnp.stack([kv_block] + [partner(kv_block, "dev", n_dev, 2 * k) for k in range(1, chips)])
    other = partner(same, "dev", n_dev, 1)
    dims = (samp_dev, n_grp, n_dev, HALVES)
    slots = []
    for half in range(HALVES):
        chosen = select(ids, sample_prompt, same, other, half, dims)
        slots.append(over_grp(chosen))

    contexts, arrived, d_queries = [], [], []
    for half in range(HALVES):
        d_q, ctx, *d_kv = attend(
            ids,
            sample_prompt,
            caption_len,
            queries[half],
            grads,
            slots[half],
            half * part,
            (samp_dev, img_len, inner, n_grp, n_dev),
        )
        d_queries.append(d_q)
        contexts.append(ctx)
        arrived.append(over_grp(d_kv))

    held = None
    for half in range(HALVES):
        held = image_product(
            d_queries[half], q_weight, contexts[half], held, half * part * img_len, rows
        )
    image_grad, context = held

    mine, theirs = combine(ids, sample_prompt, list(zip(*arrived)), dims)
    both = mine + partner(theirs, "dev", n_dev, 1).astype(F32)
    kv_grad = both[0]
    for k in range(1, chips):
        sent = partner(both[k].astype(BF16), "dev", n_dev, 2 * k)
        kv_grad = kv_grad + sent.astype(F32)
    grad_blocks = over_grp([kv_grad.astype(BF16)] * n_grp)
    shares = over_grp(project(grad_blocks, kv_weight, NT, share))
    caption_grad = jnp.zeros((block_len, width_cap), F32)
    for k in range(n_grp):
        caption_grad = lax.dynamic_update_slice_in_dim(
            caption_grad, shares[k], (grp_at ^ k) * share, 1
        )
    return (
        context.reshape(samp_dev, img_len, inner),
        image_grad.reshape(samp_dev, img_len, width_img),
        caption_grad[None],
    )


def solution(mesh):
    placed = (
        P("dev", "grp", None),
        P("grp", None),
        P(("grp", "dev"), None, None),
        P(),
        P(("grp", "dev"), None, None),
        P(),
        P(),
    )

    return jax.shard_map(
        shards,
        mesh=mesh,
        in_specs=placed,
        out_specs=(
            P(("grp", "dev"), None, None),
            P(("grp", "dev"), None, None),
            P("dev", "grp", None),
        ),
        check_vma=False,
    )
```
